512 devices in a mesh: virt: 128 (over x, y_hi, z, core), opair: 4 (over y_lo).
Axes of the slice: x: 4, y: 8 (y_hi: 2, y_lo: 4; y = y_hi * 4 + y_lo), z: 8, core: 2. Of those that a mesh axis runs over, the one named last changes fastest.
Arguments:
- amplitudes: bfloat16 [1024, 6144], P('virt', 'opair'), may hold values from -6 to 6
- integrals: bfloat16 [6144, 1024, 128], P('opair', 'virt'), may hold values from -0.078125 to 0.078125
- driver: bfloat16 [1024, 1024, 128], P('opair', 'virt'), may hold values from -6 to 6
- eps_occ: float32 [200], replicated, may hold values from -2 to -0.5
- eps_vir: float32 [1024], replicated, may hold values from 0.2 to 2
- pair_occ: int32 [1024, 2], P('opair'), may hold values from 0 to 199
- offsets: int32 [1024], P('virt'), may hold values from 0 to 896, as said below
- sizes: int32 [1024], P('virt'), may hold values from 64 to 128, as said below
Outputs:
- update: bfloat16 [1024, 1024, 128], P('opair', 'virt')
The draws below stay inside these ranges and needn't reach their ends.
Inputs may be any that keep to these rules, and one draw needn't show every extreme that they name: There are 8 irrep blocks, block k starting at k * 128; a's block starts at offsets[a], and every block is paired with some a. sizes[a] is the length of a's block; 128 is reached by some block in every draw.
All inputs are finite; a program needn't handle non-finite values.
Results may differ from the reference program's by a relative error of at most 0.001.
Values may be sent and summed in bfloat16 or wider, within the bound.
No kernel may reach another device: no remote copies, remote signals or barrier semaphores. Data moves between devices by JAX's collectives and lax.ppermute only.
A program may use at most 64 MiB of HBM per device.

```python
import jax
import jax.numpy as jnp

NVIR = 1024
NOCC = 200
BMAX = 128
NPAIR = 1024
NSLAB = 6144


def irrep_tables(key):
    base = jax.random.fold_in(key, 4242)
    count_key = jax.random.fold_in(base, 1)
    wide_key = jax.random.fold_in(base, 2)
    label_key = jax.random.fold_in(base, 3)
    counts = jax.random.randint(count_key, (8,), BMAX // 2, BMAX + 1, dtype=jnp.int32)
    widest = jax.random.randint(wide_key, (), 0, 8, dtype=jnp.int32)
    counts = jnp.where(jnp.arange(8, dtype=jnp.int32) == widest, jnp.int32(BMAX), counts)
    starts = (jnp.arange(8, dtype=jnp.int32) * BMAX).astype(jnp.int32)
    labels = jax.random.randint(label_key, (NVIR,), 0, 8, dtype=jnp.int32)
    position = jnp.arange(NVIR, dtype=jnp.int32)
    labels = jnp.where(position < 8, position, labels).astype(jnp.int32)
    return (jnp.take(starts, labels).astype(jnp.int32), jnp.take(counts, labels).astype(jnp.int32))


def draw_offsets(key, part):
    return irrep_tables(key)[0]


def draw_sizes(key, part):
    return irrep_tables(key)[1]


def with_ends(array, stream_key, least, top_value):
    extent = array.shape
    spot = [jax.random.randint(jax.random.fold_in(stream_key, axis), (), 0, extent[axis]) for axis in range(len(extent))]
    array = array.at[tuple(spot)].set(least)
    longest = extent.index(max(extent))
    spot[longest] = (spot[longest] + 1) % extent[longest]
    return array.at[tuple(spot)].set(top_value)


def block_levels(key, extent, split, smallest, high):
    def one(dim, blocks):
        draws = jax.random.uniform(jax.random.fold_in(jax.random.fold_in(key, 6), dim), (blocks,), jnp.float32, smallest / len(split), high / len(split))
        return jnp.repeat(jnp.exp(draws), extent[dim] // blocks).reshape((-1,) + (1,) * (len(extent) - dim - 1))

    gain = one(*split[0])
    for cut in split[1:]:
        gain = gain * one(*cut)
    return gain


def normal_values(key, shape, spread, limit, pieces=(), held_as=jnp.bfloat16):
    entries = spread * jax.random.normal(key, shape, jnp.float32)
    if pieces:
        entries = entries * block_levels(key, shape, pieces, -0.22, 0.18)
    return jnp.clip(entries, -limit, limit).astype(held_as)


def setup_inputs(seed: int = 0) -> dict:
    splits = jax.random.split(jax.random.key(seed), 9)
    return {
        "amplitudes": normal_values(splits[0], (NPAIR, NSLAB), 1.0, 6.0, ((0, 128), (1, 4))),
        "integrals": normal_values(splits[1], (NSLAB, NVIR, BMAX), NSLAB ** -0.5, 0.078125, ((0, 4), (1, 128))),
        "driver": normal_values(splits[2], (NPAIR, NVIR, BMAX), 1.0, 6.0, ((0, 4), (1, 128))),
        "eps_occ": jnp.clip(jax.random.uniform(splits[3], (NOCC,), jnp.float32, -2.0, -0.5), -2.0, -0.5),
        "eps_vir": jnp.clip(jax.random.uniform(splits[4], (NVIR,), jnp.float32, 0.2, 2.0), 0.2, 2.0),
        "pair_occ": with_ends(jax.random.randint(splits[5], (NPAIR, 2), 0, NOCC), jax.random.fold_in(splits[5], 1), 0, NOCC - 1).astype(jnp.int32),
        "offsets": draw_offsets(jax.random.fold_in(splits[8], 71), 0),
        "sizes": draw_sizes(jax.random.fold_in(splits[8], 71), 0),
    }


def reference(amplitudes, integrals, driver, eps_occ, eps_vir, pair_occ, offsets, sizes):
    flat = integrals.reshape(NSLAB, NVIR * BMAX)
    ladder = jnp.dot(amplitudes, flat, preferred_element_type=jnp.float32).reshape(NPAIR, NVIR, BMAX)
    pair_energy = jnp.take(eps_occ, pair_occ[:, 0]) + jnp.take(eps_occ, pair_occ[:, 1])
    column = jnp.arange(BMAX, dtype=jnp.int32)
    b_index = (offsets[:, None] + jnp.minimum(column[None, :], sizes[:, None] - 1)).astype(jnp.int32)
    e_pair = jnp.take(eps_vir, b_index)
    denominator = pair_energy[:, None, None] - eps_vir[None, :, None] - e_pair[None, :, :]
    value = (ladder + driver.astype(jnp.float32)) / denominator
    inside = column[None, None, :] < sizes[None, :, None]
    return jnp.where(inside, value, jnp.zeros_like(value)).astype(jnp.bfloat16)
```

```python
import jax
import jax.numpy as jnp
from jax import lax
from jax.sharding import Mesh
from jax.sharding import PartitionSpec as P


VIRT = ("x", "yh", "z", "c")
NZ = 8
PIECES = ((0, 1, -1), (2, -2, 3, -3, 4))


def ring(n, step):
    return [(i, (i + step) % n) for i in range(n)]


def everywhere(block, axes, members):
    return lax.all_to_all(jnp.broadcast_to(block[None], (members,) + block.shape), axes, 0, 0)


def reduce_piece(first, second, third, ends):
    q1 = lax.ppermute(first, "yl", [(0, 1), (1, 0), (2, 3), (3, 2)])
    q2 = lax.ppermute(second, "yl", [(1, 2), (2, 1)])
    q3 = lax.ppermute(third, "yl", [(0, 2), (3, 1)])
    q4 = lax.ppermute(second, "yl", [(0, 1), (3, 2)])
    q5 = lax.ppermute(third + q1, "yl", [(1, 3), (2, 0)])
    return jnp.where(ends, q1, 0.0) + q2 + q3 + q4 + q5


def local(amplitudes, integrals, driver, eps_occ, eps_vir, pair_occ, offsets, sizes):
    slab_rows, a_count, bwidth = integrals.shape
    own_rows = driver.shape[0]
    flat = integrals.reshape(slab_rows, a_count * bwidth)
    yl = lax.axis_index("yl")
    z = lax.axis_index("z")
    ends = (yl == 0) | (yl == 3)
    slots = [jnp.array(s, jnp.int32)[yl] for s in ((3, 0, 3, 0), (1, 2, 1, 2), (2, 3, 0, 1), (0, 1, 2, 3))]

    held = everywhere(amplitudes, ("yh", "c"), 4).reshape(-1, slab_rows)
    blocks = {0: everywhere(held, "x", 4)}
    for k in range(1, 4):
        blocks[k] = lax.ppermute(blocks[k - 1], "z", ring(NZ, -1))
        blocks[-k] = lax.ppermute(blocks[1 - k], "z", ring(NZ, 1))
    blocks[4] = lax.ppermute(blocks[3], "z", ring(NZ, -1))
    unit = held.shape[0]

    pair_energy = jnp.take(eps_occ, pair_occ[:, 0]) + jnp.take(eps_occ, pair_occ[:, 1])
    column = jnp.arange(bwidth, dtype=jnp.int32)
    b_index = offsets[:, None] + jnp.minimum(column[None, :], sizes[:, None] - 1)
    e_pair = jnp.take(eps_vir, b_index)
    first_a = ((lax.axis_index("x") * 2 + lax.axis_index("yh")) * NZ + z) * 2 + lax.axis_index("c")
    e_first = lax.dynamic_slice_in_dim(eps_vir, first_a * a_count, a_count, 0)
    inside = column[None, :] < sizes[:, None]

    def rel(array):
        rest = array.shape[1:]
        parts = array.reshape((2, NZ, unit // 2) + rest)
        parts = lax.dynamic_slice_in_dim(jnp.concatenate([parts, parts], axis=1), z, NZ, 1)
        return jnp.swapaxes(parts, 0, 1).reshape((NZ, unit) + rest)

    driver_rel = rel(driver)
    energy_rel = rel(pair_energy)

    results = {}
    for piece in PIECES:
        dots = []
        for s in slots:
            rows = jnp.concatenate([lax.dynamic_index_in_dim(blocks[k], s, 0, keepdims=False) for k in piece], axis=0)
            dots.append(jnp.dot(rows, flat, preferred_element_type=jnp.float32))
        others = reduce_piece(dots[0], dots[1], dots[2], ends)
        ladder = (dots[3] + others).reshape(len(piece), unit, a_count, bwidth)
        which = [k % NZ for k in piece]
        drv = jnp.stack([driver_rel[k] for k in which])
        energy = jnp.stack([energy_rel[k] for k in which])
        denominator = energy[:, :, None, None] - e_first[None, None, :, None] - e_pair[None, None]
        value = (ladder + drv.astype(jnp.float32)) / denominator
        value = jnp.where(inside[None, None], value, jnp.zeros_like(value)).astype(jnp.bfloat16)
        for i, k in enumerate(which):
            results[k] = value[i]
    out = jnp.stack([results[k] for k in range(NZ)])
    out = jnp.swapaxes(out.reshape((NZ, 2, unit // 2, a_count, bwidth)), 0, 1)
    out = lax.dynamic_slice_in_dim(jnp.concatenate([out, out], axis=1), (NZ - z) % NZ, NZ, 1)
    return out.reshape(own_rows, a_count, bwidth)


def solution(mesh):
    fine = Mesh(mesh.devices.reshape(4, 2, 8, 2, 4), ("x", "yh", "z", "c", "yl"))
    placed = (
        P(VIRT, "yl"),
        P("yl", VIRT, None),
        P("yl", VIRT, None),
        P(),
        P(),
        P("yl", None),
        P(VIRT),
        P(VIRT),
    )
    return jax.shard_map(
        local, mesh=fine, in_specs=placed, out_specs=P("yl", VIRT, None), check_vma=False
    )
```

```python
import jax
import jax.numpy as jnp
from jax import lax
from jax.experimental import pallas as pl
from jax.experimental.pallas import tpu as pltpu
from jax.sharding import Mesh
from jax.sharding import PartitionSpec as P


VIRT = ("x", "yh", "z", "c")
NZ = 8
PIECES = ((0, 1, -1), (2, -2, 3, -3, 4))


def ring(n, step):
    return [(i, (i + step) % n) for i in range(n)]


def everywhere(block, axes, members):
    return lax.all_to_all(jnp.broadcast_to(block[None], (members,) + block.shape), axes, 0, 0)


def exchange(first, second, third):
    q1 = lax.ppermute(first, "yl", [(0, 1), (1, 0), (2, 3), (3, 2)])
    q2 = lax.ppermute(second, "yl", [(1, 2), (2, 1)])
    q3 = lax.ppermute(third, "yl", [(0, 2), (3, 1)])
    q5 = lax.ppermute(third + q1, "yl", [(1, 3), (2, 0)])
    q4 = lax.ppermute(second, "yl", [(0, 1), (3, 2)])
    return q1, q2, q3, q4, q5


def finish(table, own, q1, q2, q3, q4, q5, driver, energy, e_first, e_pair, width, *rest):
    out = rest[-1]
    shape = driver.shape
    ends = table[NZ] == 1
    others = q2[...] + q3[...] + q4[...] + q5[...] + jnp.where(ends, q1[...], 0.0)
    ladder = (own[...] + others).reshape(own.shape[0], shape[3], shape[4])
    terms = driver[...].reshape(ladder.shape).astype(jnp.float32)
    denominator = energy[...].reshape(own.shape[0], 1, 1) - e_first[...][None] - e_pair[...][None]
    value = (ladder + terms) / denominator
    column = lax.broadcasted_iota(jnp.int32, e_pair.shape, 1)
    value = jnp.where((column < width[...])[None], value, 0.0)
    out[...] = value.astype(out.dtype).reshape(shape)


def update(table, own, received, driver, energy, e_first, e_pair, width, count, so_far):
    unit = own.shape[0] // count
    rows = pl.BlockSpec((unit, own.shape[1]), lambda i, t: (i, 0))
    block = (2, 1) + driver.shape[2:]
    placed = pl.BlockSpec(block, lambda i, t: (0, t[i], 0, 0, 0))
    whole = lambda a: pl.BlockSpec(a.shape, lambda i, t: (0,) * a.ndim)
    inputs = [own, *received, driver, energy, e_first, e_pair, width]
    specs = [rows] * 6 + [placed, pl.BlockSpec((2, 1, unit // 2, 1), lambda i, t: (0, t[i], 0, 0))]
    specs += [whole(e_first), whole(e_pair), whole(width)]
    aliases = {}
    if so_far is not None:
        aliases = {len(inputs) + 1: 0}
        inputs.append(so_far)
        specs.append(pl.BlockSpec(memory_space=pl.ANY))
    return pl.pallas_call(
        finish,
        out_shape=jax.ShapeDtypeStruct(driver.shape, jnp.bfloat16),
        grid_spec=pltpu.PrefetchScalarGridSpec(
            num_scalar_prefetch=1, grid=(count,), in_specs=specs, out_specs=placed
        ),
        input_output_aliases=aliases,
        cost_estimate=pl.CostEstimate(flops=own.size * 12, bytes_accessed=own.size * 28, transcendentals=0),
    )(table, *inputs)


def local(amplitudes, integrals, driver, eps_occ, eps_vir, pair_occ, offsets, sizes):
    slab_rows, a_count, bwidth = integrals.shape
    own_rows = driver.shape[0]
    flat = integrals.reshape(slab_rows, a_count * bwidth)
    yl = lax.axis_index("yl")
    z = lax.axis_index("z")
    odd = yl % 2
    slots = (3 - 3 * odd, 1 + odd, (yl + 2) % 4, yl)

    held = everywhere(amplitudes, ("yh", "c"), 4).reshape(-1, slab_rows)
    blocks = {0: everywhere(held, "x", 4)}
    for k in range(1, 4):
        blocks[k] = lax.ppermute(blocks[k - 1], "z", ring(NZ, -1))
        blocks[-k] = lax.ppermute(blocks[1 - k], "z", ring(NZ, 1))
    blocks[4] = lax.ppermute(blocks[3], "z", ring(NZ, -1))
    unit = held.shape[0]

    index = jnp.arange(eps_occ.shape[0], dtype=jnp.int32)[:, None]
    pick = lambda i: jnp.sum(jnp.where(index == pair_occ[:, i][None, :], eps_occ[:, None], 0.0), axis=0)
    energy = (pick(0) + pick(1)).reshape(2, NZ, unit // 2, 1)
    table = eps_vir.reshape(-1, bwidth)
    start = jnp.arange(table.shape[0], dtype=jnp.int32) * bwidth
    e_pair = jnp.sum(jnp.where(offsets[:, None, None] == start[None, :, None], table[None], 0.0), axis=1)
    first_a = ((lax.axis_index("x") * 2 + lax.axis_index("yh")) * NZ + z) * 2 + lax.axis_index("c")
    e_first = lax.dynamic_slice_in_dim(eps_vir, first_a * a_count, a_count, 0)[:, None]
    width = sizes[:, None]
    driver = driver.reshape(2, NZ, unit // 2, a_count, bwidth)
    ends = ((yl == 0) | (yl == 3)).astype(jnp.int32)

    out = None
    for piece in PIECES:
        dots = []
        for s in slots:
            rows = jnp.concatenate([lax.dynamic_index_in_dim(blocks[k], s, 0, keepdims=False) for k in piece], axis=0)
            dots.append(jnp.dot(rows, flat, preferred_element_type=jnp.float32))
        received = exchange(*dots[:3])
        shift = jnp.array([k % NZ for k in piece] + [0] * (NZ - len(piece)), jnp.int32)
        places = jnp.concatenate([(shift + z) % NZ, ends[None]])
        out = update(places, dots[3], received, driver, energy, e_first, e_pair, width, len(piece), out)
    return out.reshape(own_rows, a_count, bwidth)


def solution(mesh):
    fine = Mesh(mesh.devices.reshape(4, 2, 8, 2, 4), ("x", "yh", "z", "c", "yl"))
    placed = (
        P(VIRT, "yl"),
        P("yl", VIRT, None),
        P("yl", VIRT, None),
        P(),
        P(),
        P("yl", None),
        P(VIRT),
        P(VIRT),
    )
    return jax.shard_map(
        local, mesh=fine, in_specs=placed, out_specs=P("yl", VIRT, None), check_vma=False
    )
```

```python
import jax
import jax.numpy as jnp
from jax import lax
from jax.experimental import pallas as pl
from jax.experimental.pallas import tpu as pltpu
from jax.sharding import Mesh
from jax.sharding import PartitionSpec as P


VIRT = ("x", "yh", "z", "c")
NZ = 8
PIECES = ((0,), (1, 7), (2, 6), (3, 5), (4,))


def ring(n, step):
    return [(i, (i + step) % n) for i in range(n)]


def everywhere(block, axes, members):
    return lax.all_to_all(jnp.broadcast_to(block[None], (members,) + block.shape), axes, 0, 0)


def finish(place, own, near, far, driver, energy, e_first, e_pair, width, *rest):
    out = rest[-1]
    shape = driver.shape
    ladder = (own[...] + near[...] + far[...]).reshape(own.shape[0], shape[3], shape[4])
    terms = driver[...].reshape(ladder.shape).astype(jnp.float32)
    denominator = energy[...].reshape(own.shape[0], 1, 1) - e_first[...][None] - e_pair[...][None]
    value = (ladder + terms) / denominator
    column = lax.broadcasted_iota(jnp.int32, e_pair.shape, 1)
    value = jnp.where((column < width[...])[None], value, 0.0)
    out[...] = value.astype(out.dtype).reshape(shape)


def update(place, piece, own, near, far, driver, energy, e_first, e_pair, width, so_far):
    count = len(piece)
    unit = own.shape[0] // count
    at = lambda i, t: (t[0] + sum(jnp.where(i == j, k, 0) for j, k in enumerate(piece))) % NZ
    rows = pl.BlockSpec((unit, own.shape[1]), lambda i, t: (i, 0))
    second = pl.BlockSpec((unit, own.shape[1]), lambda i, t: (i + count, 0))
    placed = pl.BlockSpec((2, 1) + driver.shape[2:], lambda i, t: (0, at(i, t), 0, 0, 0))
    whole = lambda a: pl.BlockSpec(a.shape, lambda i, t: (0,) * a.ndim)
    driver = pltpu.with_memory_space_constraint(driver, pltpu.HBM)
    inputs = [own, near, far, driver, energy, e_first, e_pair, width]
    specs = [rows, second, rows, placed, pl.BlockSpec((2, 1, unit // 2, 1), lambda i, t: (0, at(i, t), 0, 0))]
    specs += [whole(e_first), whole(e_pair), whole(width)]
    aliases = {}
    if so_far is not None:
        aliases = {len(inputs) + 1: 0}
        inputs.append(so_far)
        specs.append(pl.BlockSpec(memory_space=pl.ANY))
    return pl.pallas_call(
        finish,
        out_shape=jax.ShapeDtypeStruct(driver.shape, jnp.bfloat16),
        grid_spec=pltpu.PrefetchScalarGridSpec(
            num_scalar_prefetch=1, grid=(count,), in_specs=specs, out_specs=placed
        ),
        input_output_aliases=aliases,
        compiler_params=pltpu.CompilerParams(vmem_limit_bytes=8 << 20),
        cost_estimate=pl.CostEstimate(flops=own.size * 12, bytes_accessed=own.size * 16, transcendentals=0),
    )(place, *inputs)


def products(*refs):
    *blocks, flat, away, onward, own = refs
    rows = jnp.concatenate([b[i] for i in range(4) for b in blocks])
    value = jnp.dot(rows, flat[...], preferred_element_type=jnp.float32)
    n = own.shape[0]
    away[...] = value[: 2 * n]
    onward[...] = value[2 * n : 3 * n]
    own[...] = value[3 * n :]


def partial_sums(blocks, flat, tile=256):
    depth, columns = flat.shape
    n = blocks[0].shape[1] * len(blocks)
    out = lambda m: pl.BlockSpec((m, tile), lambda i: (0, i))
    return pl.pallas_call(
        products,
        out_shape=[jax.ShapeDtypeStruct((m, columns), jnp.float32) for m in (2 * n, n, n)],
        grid=(columns // tile,),
        in_specs=[pl.BlockSpec(b.shape, lambda i: (0, 0, 0)) for b in blocks]
        + [pl.BlockSpec((depth, tile), lambda i: (0, i))],
        out_specs=[out(2 * n), out(n), out(n)],
        compiler_params=pltpu.CompilerParams(vmem_limit_bytes=12 << 20),
        cost_estimate=pl.CostEstimate(flops=8 * n * depth * columns, bytes_accessed=4 << 20, transcendentals=0),
    )(*blocks, flat)


def step(amplitudes, integrals, driver, eps_occ, eps_vir, pair_occ, offsets, sizes):
    slab_rows, a_count, bwidth = integrals.shape
    own_rows = driver.shape[0]
    flat = integrals.reshape(slab_rows, a_count * bwidth)
    yl = lax.axis_index("yl")
    z = lax.axis_index("z")
    held = everywhere(amplitudes, ("yh", "c"), 4).reshape(-1, slab_rows)
    planes = everywhere(held, "x", 4)
    blocks = {0: jnp.stack([lax.dynamic_index_in_dim(planes, yl ^ k, 0, keepdims=False) for k in (3, 1, 2, 0)])}
    for k in range(1, 5):
        blocks[k] = lax.ppermute(blocks[k - 1], "z", ring(NZ, -1))
        if k < 4:
            blocks[NZ - k] = lax.ppermute(blocks[(1 - k) % NZ], "z", ring(NZ, 1))
    unit = held.shape[0]

    index = jnp.arange(eps_occ.shape[0], dtype=jnp.int32)[:, None]
    pick = lambda i: jnp.sum(jnp.where(index == pair_occ[:, i][None, :], eps_occ[:, None], 0.0), axis=0)
    energy = (pick(0) + pick(1)).reshape(2, NZ, unit // 2, 1)
    table = eps_vir.reshape(-1, bwidth)
    start = jnp.arange(table.shape[0], dtype=jnp.int32) * bwidth
    e_pair = jnp.sum(jnp.where(offsets[:, None, None] == start[None, :, None], table[None], 0.0), axis=1)
    first_a = ((lax.axis_index("x") * 2 + lax.axis_index("yh")) * NZ + z) * 2 + lax.axis_index("c")
    e_first = lax.dynamic_slice_in_dim(eps_vir, first_a * a_count, a_count, 0)[:, None]
    width = sizes[:, None]
    driver = driver.reshape(2, NZ, unit // 2, a_count, bwidth)

    out = None
    for piece in PIECES:
        away, onward, own = partial_sums([blocks[k] for k in piece], flat)
        near = lax.ppermute(away, "yl", [(0, 1), (1, 0), (2, 3), (3, 2)])
        onward = onward + near[: onward.shape[0]]
        far = lax.ppermute(onward, "yl", [(0, 2), (2, 0), (1, 3), (3, 1)])
        out = update(z[None], piece, own, near, far, driver, energy, e_first, e_pair, width, out)
    return out.reshape(own_rows, a_count, bwidth)


def solution(mesh):
    fine = Mesh(mesh.devices.reshape(4, 2, 8, 2, 4), ("x", "yh", "z", "c", "yl"))
    placed = (
        P(VIRT, "yl"),
        P("yl", VIRT, None),
        P("yl", VIRT, None),
        P(),
        P(),
        P("yl", None),
        P(VIRT),
        P(VIRT),
    )
    return jax.shard_map(step, mesh=fine, in_specs=placed, out_specs=P("yl", VIRT, None), check_vma=False)
```
